256 devices in a mesh: row: 4 (over y), col: 32 (over x_lo, z, core), feat: 2 (over x_hi).
Axes of the slice: x: 4 (x_hi: 2, x_lo: 2; x = x_hi * 2 + x_lo), y: 4, z: 8, core: 2. Of those that a mesh axis runs over, the one named last changes fastest.
Arguments:
- panel_student: bfloat16 [2048, 4096], P('row', 'feat'), may hold values from -0.01171875 to 0.01171875
- panel_teacher: bfloat16 [2048, 4096], P('row', 'feat'), may hold values from -0.01171875 to 0.01171875
- tokens_student: bfloat16 [24576, 4096], P('col', 'feat'), may hold values from -0.01171875 to 0.01171875
- tokens_teacher: bfloat16 [24576, 4096], P('col', 'feat'), may hold values from -0.01171875 to 0.01171875
Outputs:
- row_loss: float32 [2048], P(('row', 'col'))
- grad_panel: bfloat16 [2048, 4096], P(('row', 'col'), 'feat')
- grad_tokens: bfloat16 [24576, 4096], P('col', 'feat')
The draws below stay inside these ranges and needn't reach their ends.
All inputs are finite; a program needn't handle non-finite values.
Results may differ from the reference program's by a relative error of at most 0.0058.
Values may be sent and summed in bfloat16 or wider, within the bound.
No kernel may reach another device: no remote copies, remote signals or barrier semaphores. Data moves between devices by JAX's collectives and lax.ppermute only.
A program may use at most 128 MiB of HBM per device.

```python
import jax
import jax.numpy as jnp
from jax import lax

D = 4096
PANEL = 2048
TOKENS = 24576


def block_levels(key, extent, shards, least, high):
    level, own = 1.0, jax.random.fold_in(key, 6)
    for position, parts in shards:
        draws = jnp.exp(jax.random.uniform(jax.random.fold_in(own, position), (parts,), jnp.float32, least / len(shards), high / len(shards)))
        level = level * jnp.repeat(draws, extent[position] // parts).reshape([-1 if axis == position else 1 for axis in range(len(extent))])
    return level


def noise(key, extent, spread, limit, cuts=(), held_as=jnp.bfloat16):
    array = spread * jax.random.normal(key, extent, jnp.float32)
    if cuts:
        array = array * block_levels(key, extent, cuts, -0.22, 0.18)
    return jnp.clip(array, -limit, limit).astype(held_as)


def setup_inputs(seed: int = 0) -> dict:
    keys = jax.random.split(jax.random.key(seed), 5)
    panel_student = noise(keys[0], (PANEL, D), 0.001953125, 0.01171875, ((0, 4), (1, 2)))
    panel_teacher = noise(keys[1], (PANEL, D), 0.001953125, 0.01171875, ((0, 4), (1, 2)))
    tokens_student = noise(keys[2], (TOKENS, D), 0.001953125, 0.01171875, ((0, 32), (1, 2)))
    tokens_teacher = noise(keys[3], (TOKENS, D), 0.001953125, 0.01171875, ((0, 32), (1, 2)))
    return dict(panel_student=panel_student, panel_teacher=panel_teacher, tokens_student=tokens_student, tokens_teacher=tokens_teacher)


epsilon = 1e-06

def inverse_norm(features):
    values = features.astype(jnp.float32)
    return 1.0 / jnp.sqrt(lax.optimization_barrier(jnp.sum(values * values, axis=1)) + epsilon)

def finish(term, unit, inverse):
    along = lax.optimization_barrier(jnp.sum(unit * term, axis=1))
    return ((term - unit * along[:, None]) * inverse[:, None]).astype(jnp.bfloat16)

def reference(panel_student, panel_teacher, tokens_student, tokens_teacher):
    inv_ps = inverse_norm(panel_student)
    inv_pt = inverse_norm(panel_teacher)
    inv_ts = inverse_norm(tokens_student)
    inv_tt = inverse_norm(tokens_teacher)
    student_gram = jnp.dot(panel_student, tokens_student.T, preferred_element_type=jnp.float32) * inv_ps[:, None] * inv_ts[None, :]
    teacher_gram = jnp.dot(panel_teacher, tokens_teacher.T, preferred_element_type=jnp.float32) * inv_pt[:, None] * inv_tt[None, :]
    mismatch = student_gram - teacher_gram
    row_loss = lax.optimization_barrier(jnp.sum(mismatch * mismatch, axis=1))
    doubled = (2.0 * mismatch).astype(jnp.bfloat16)
    panel_unit = panel_student.astype(jnp.float32) * inv_ps[:, None]
    token_unit = tokens_student.astype(jnp.float32) * inv_ts[:, None]
    panel_half = panel_unit.astype(jnp.bfloat16)
    token_half = token_unit.astype(jnp.bfloat16)
    panel_term = jnp.dot(doubled, token_half, preferred_element_type=jnp.float32)
    token_term = jnp.dot(doubled.T, panel_half, preferred_element_type=jnp.float32)
    grad_panel = finish(panel_term, panel_unit, inv_ps)
    grad_tokens = finish(token_term, token_unit, inv_tt * 0.0 + inv_ts)
    return (row_loss, grad_panel, grad_tokens)
```

```python
import jax
import jax.numpy as jnp
from jax import lax
from jax.experimental import pallas as pl
from jax.experimental.pallas import tpu as pltpu
from jax.sharding import PartitionSpec as P


epsilon = 1e-06
bf16, f32 = jnp.bfloat16, jnp.float32
SMEM = pl.BlockSpec(memory_space=pltpu.SMEM)


def row_shift(x, by):
    return lax.ppermute(x, "row", [(i, (i + by) % 4) for i in range(4)])


def feat_swap(x):
    return lax.ppermute(x, "feat", [(0, 1), (1, 0)])


def col_move(x, move):
    def target(c):
        a, z, k = move(c // 16, (c // 2) % 8, c % 2)
        return a * 16 + z * 2 + k

    return lax.ppermute(x, "col", [(c, target(c)) for c in range(32)])


def core_swap(x):
    return col_move(x, lambda a, z, k: (a, z, 1 - k))


def deep_shift(x, by):
    return col_move(x, lambda a, z, k: (a, (z + by) % 8, k))


def fold_lanes(x):
    return sum(x[:, i : i + 128] for i in range(0, x.shape[1], 128))


def to_row(x):
    return jnp.sum(x.T, axis=0, keepdims=True)


def column(row, copies):
    tall = jnp.broadcast_to(row, (128, row.shape[1])).T
    return jnp.concatenate([tall] * copies, axis=1)


def shape(dims, dtype):
    return jax.ShapeDtypeStruct(dims, dtype)


def gram_kernel(ps, pt, ts, tt, student, teacher, sums, squares):
    step = pl.program_id(0)

    def inner(left, right):
        return lax.dot_general(left[...], right[...], (((1,), (1,)), ((), ())), preferred_element_type=f32)

    @pl.when(step == 0)
    def _():
        student[...] = jnp.zeros_like(student)
        teacher[...] = jnp.zeros_like(teacher)
        squares[...] = jnp.zeros_like(squares)

    student[...] += inner(ts, ps)
    teacher[...] += inner(tt, pt)
    start = 0
    for ref in (ps, pt, ts, tt):
        values = ref[...].astype(f32)
        rows = slice(start, start + values.shape[0])
        squares[rows] += fold_lanes(values * values)
        start += values.shape[0]

    @pl.when(step == pl.num_programs(0) - 1)
    def _():
        sums[...] = to_row(squares[...])


def grams(ps, pt, ts, tt):
    block = 512
    strip = lambda a: pl.BlockSpec((a.shape[0], block), lambda i: (0, i))
    same = lambda *dims: pl.BlockSpec(dims, lambda i: (0, 0))
    return pl.pallas_call(
        gram_kernel,
        grid=(ps.shape[1] // block,),
        out_shape=[shape((768, 512), f32), shape((768, 512), f32), shape((1, 2560), f32)],
        in_specs=[strip(a) for a in (ps, pt, ts, tt)],
        out_specs=[same(768, 512), same(768, 512), same(1, 2560)],
        scratch_shapes=[pltpu.VMEM((2560, 128), f32)],
        name="grams",
    )(ps, pt, ts, tt)


def inverses(mine, other):
    invs = 1.0 / jnp.sqrt(mine[...] + other[...] + epsilon)
    return invs[:, :512], invs[:, 512:1024], invs[:, 1024:1792], invs[:, 1792:]


def scaled(student, teacher, mine, other):
    inv_ps, inv_pt, inv_ts, inv_tt = inverses(mine, other)
    tall = column(inv_ts, 4)
    near = student[...] * inv_ps * tall
    return near, near - teacher[...] * inv_pt * column(inv_tt, 4), inv_ps, tall


def part_kernel(student, teacher, mine, other, out):
    out[...] = scaled(student, teacher, mine, other)[1].astype(bf16)


def mismatch_kernel(student, teacher, mine, other, partner, doubled, weighted, loss, along):
    near, part, inv_ps, tall = scaled(student, teacher, mine, other)
    mismatch = part + partner[...].astype(f32)
    twice = 2.0 * mismatch
    doubled[...] = (twice * inv_ps).astype(bf16)
    weighted[...] = (twice * tall).astype(bf16)
    loss[...] = column(jnp.sum(mismatch * mismatch, axis=0, keepdims=True), 1)
    along[...] = to_row(fold_lanes(twice * near))


def split_pair(total):
    lane = lax.broadcasted_iota(jnp.int32, total.shape, total.ndim - 1)
    high = total.astype(bf16).astype(f32)
    return jnp.where(lane == 0, high, jnp.where(lane == 1, total - high, 0.0))


def panel_kernel(core, weighted, ts, loss, away, keep, work):
    product = lax.dot_general(weighted[...], ts[...], (((0,), (0,)), ((), ())), preferred_element_type=f32)
    work[:, :, :, :2048] = product.reshape(16, 2, 16, 2048)
    work[:, :, :, 2048:] = loss[...].reshape(16, 2, 16, 128)
    other = work[:, 1 - core[0]]
    away[:, :, :2048] = other[:, :, :2048].astype(bf16)
    away[:, :, 2048:] = split_pair(other[:, :, 2048:]).astype(bf16)
    own = work[:, core[0]]
    lane = lax.broadcasted_iota(jnp.int32, (16, 16, 128), 2)
    keep[:, :, :2048] = own[:, :, :2048]
    keep[:, :, 2048:] = jnp.where(lane == 0, own[:, :, 2048:], 0.0)


def join_kernel(keep, away, out):
    out[:, :, :2048] = (keep[:, :, :2048] + away[:, :, :2048].astype(f32)).astype(bf16)
    total = jnp.sum(keep[:, :, 2048:] + away[:, :, 2048:].astype(f32), axis=2, keepdims=True)
    out[:, :, 2048:] = split_pair(jnp.broadcast_to(total, (16, 16, 128))).astype(bf16)


def token_kernel(place, d0, dl, dr, do, ps, *refs):
    pieces, (ts, mine, other, along, out, work) = refs[:12], refs[12:]
    deep, core = place[0], place[1]
    for order, (a, b) in enumerate(((deep, core), (1 - deep, core), (deep, 1 - core), (1 - deep, 1 - core))):
        start = pl.multiple_of((a * 2 + b) * 128, 128)
        for side in range(3):
            work[side, pl.ds(start, 128)] = pieces[order * 3 + side][...]

    def dot(a, b):
        return jnp.dot(a, b, preferred_element_type=f32)

    total = dot(d0[...], ps[...]) + dot(dl[...], work[0]) + dot(dr[...], work[1]) + dot(do[...], work[2])
    inv_ts = inverses(mine, other)[2]
    copies = ts.shape[1] // 128
    scale = column(inv_ts, copies)
    shade = column(inv_ts * inv_ts * along[...], copies)
    out[...] = (total * scale - ts[...].astype(f32) * shade).astype(bf16)


def token_grad(place, doubled, ps, pieces, ts, mine, other, along):
    rows, width = ts.shape
    block = 512
    whole = lambda a: pl.BlockSpec(a.shape, lambda i: (0, 0))
    strip = lambda a: pl.BlockSpec((a.shape[0], block), lambda i: (0, i))
    return pl.pallas_call(
        token_kernel,
        grid=(width // block,),
        out_shape=shape((rows, width), bf16),
        in_specs=[SMEM]
        + [whole(a) for a in doubled]
        + [strip(a) for a in (ps, *pieces, ts)]
        + [whole(a) for a in (mine, other, along)],
        out_specs=pl.BlockSpec((rows, block), lambda i: (0, i)),
        scratch_shapes=[pltpu.VMEM((3, 512, block), bf16)],
        name="tokens",
    )(place, *doubled, ps, *pieces, ts, mine, other, along)


def local(panel_student, panel_teacher, tokens_student, tokens_teacher):
    col = lax.axis_index("col")
    deep, core = (col // 2) % 2, col % 2
    place = jnp.stack([deep, core]).astype(jnp.int32)

    quarter = lax.dynamic_slice_in_dim(panel_student, (deep * 2 + core) * 128, 128, 0)
    left = row_shift(quarter, 1)
    right = row_shift(quarter, 3)
    far = row_shift(quarter, 2)
    first = (left, right, far)
    second = (deep_shift(left, 1), deep_shift(right, 7), deep_shift(far, 1))
    third = tuple(core_swap(a) for a in first)
    fourth = tuple(core_swap(a) for a in second)
    pieces = first + second + third + fourth

    student, teacher, mine = grams(panel_student, panel_teacher, tokens_student, tokens_teacher)
    other = feat_swap(mine)
    part = pl.pallas_call(part_kernel, out_shape=shape((768, 512), bf16), name="part")(student, teacher, mine, other)
    partner = feat_swap(part)
    doubled, weighted, loss, along = pl.pallas_call(
        mismatch_kernel,
        out_shape=[shape((768, 512), bf16), shape((768, 512), bf16), shape((512, 128), f32), shape((1, 768), f32)],
        name="mismatch",
    )(student, teacher, mine, other, partner)
    gathered = (doubled, row_shift(doubled, 1), row_shift(doubled, 3), row_shift(doubled, 2))

    away, keep = pl.pallas_call(
        panel_kernel,
        out_shape=[shape((16, 16, 2176), bf16), shape((16, 16, 2176), f32)],
        in_specs=[SMEM] + [pl.BlockSpec(memory_space=pltpu.VMEM)] * 3,
        scratch_shapes=[pltpu.VMEM((16, 2, 16, 2176), f32)],
        name="panel",
    )(place[1:], weighted, tokens_student, loss)
    away = core_swap(away)

    along += feat_swap(along)
    along += row_shift(along, 1)
    along += row_shift(along, 2)

    joined = pl.pallas_call(join_kernel, out_shape=shape((16, 16, 2176), bf16), name="join")(keep, away)
    groups = [[a * 16 + z * 2 + k for a in range(2) for z in range(8)] for k in range(2)]
    spread = lax.all_to_all(joined, "col", 0, 0, axis_index_groups=groups, tiled=True)

    total = jnp.sum(spread.astype(f32), axis=0)
    panel_term = total[:, :2048]
    row_loss = total[:, 2048] + total[:, 2049]
    rows = lambda a: lax.dynamic_slice_in_dim(a, col * 16, 16, 0)
    inv_rows = 1.0 / jnp.sqrt(rows(mine[0]) + rows(other[0]) + epsilon)
    unit = rows(panel_student).astype(f32) * inv_rows[:, None]
    along_rows = jnp.sum(unit * panel_term, axis=1)
    along_rows += feat_swap(along_rows)
    grad_tokens = token_grad(place, gathered, panel_student, pieces, tokens_student, mine, other, along)
    grad_panel = ((panel_term - unit * along_rows[:, None]) * inv_rows[:, None]).astype(bf16)
    return (row_loss, grad_panel, grad_tokens)


def solution(mesh):
    placed = (P("row", "feat"), P("row", "feat"), P("col", "feat"), P("col", "feat"))
    return jax.shard_map(
        local,
        mesh=mesh,
        in_specs=placed,
        out_specs=(P(("row", "col")), P(("row", "col"), "feat"), P("col", "feat")),
        check_vma=False,
    )
```

```python
import jax
import jax.numpy as jnp
from jax import lax
from jax.experimental import pallas as pl
from jax.experimental.pallas import tpu as pltpu
from jax.sharding import PartitionSpec as P


epsilon = 1e-06
bf16, f32 = jnp.bfloat16, jnp.float32
SMEM = pl.BlockSpec(memory_space=pltpu.SMEM)


def row_shift(x, by):
    return lax.ppermute(x, "row", [(i, (i + by) % 4) for i in range(4)])


def feat_swap(x):
    return lax.ppermute(x, "feat", [(0, 1), (1, 0)])


def col_move(x, move):
    def target(c):
        a, z, k = move(c // 16, (c // 2) % 8, c % 2)
        return a * 16 + z * 2 + k

    return lax.ppermute(x, "col", [(c, target(c)) for c in range(32)])


def core_swap(x):
    return col_move(x, lambda a, z, k: (a, z, 1 - k))


def deep_shift(x, by):
    return col_move(x, lambda a, z, k: (a, (z + by) % 8, k))


def fold_lanes(x):
    return sum(x[:, i : i + 128] for i in range(0, x.shape[1], 128))


def to_row(x):
    return jnp.sum(x.T, axis=0, keepdims=True)


def column(row, copies):
    tall = jnp.broadcast_to(row, (128, row.shape[1])).T
    return jnp.concatenate([tall] * copies, axis=1)


def shape(dims, dtype):
    return jax.ShapeDtypeStruct(dims, dtype)


def norm_kernel(ps, pt, ts, tt, sums, squares):
    step = pl.program_id(0)

    @pl.when(step == 0)
    def _():
        squares[...] = jnp.zeros_like(squares)

    start = 0
    for ref in (ps, pt, ts, tt):
        values = ref[...].astype(f32)
        rows = slice(start, start + values.shape[0])
        squares[rows] += fold_lanes(values * values)
        start += values.shape[0]

    @pl.when(step == pl.num_programs(0) - 1)
    def _():
        sums[...] = to_row(squares[...])


def strip(a, width=512, last=None):
    if last is None:
        return pl.BlockSpec((a.shape[0], width), lambda i: (0, i))
    return pl.BlockSpec((a.shape[0], width), lambda i: (0, jnp.minimum(i, last)))


def whole(a):
    return pl.BlockSpec(a.shape, lambda i: (0,) * len(a.shape))


def norms(*features):
    return pl.pallas_call(
        norm_kernel,
        grid=(4,),
        out_shape=shape((1, 2560), f32),
        in_specs=[strip(a) for a in features],
        out_specs=pl.BlockSpec((1, 2560), lambda i: (0, 0)),
        scratch_shapes=[pltpu.VMEM((2560, 128), f32)],
        name="norms",
    )(*features)


def gram_kernel(ps, pt, ts, tt, student, teacher):
    def inner(left, right):
        return lax.dot_general(left[...], right[...], (((1,), (1,)), ((), ())), preferred_element_type=f32)

    student[...] = inner(ts, ps)
    teacher[...] = inner(tt, pt)


def tall(width):
    return pl.BlockSpec((256, width), lambda i: (i, 0))


def grams(ps, pt, ts, tt):
    return pl.pallas_call(
        gram_kernel,
        grid=(3,),
        out_shape=[shape((768, 512), f32)] * 2,
        in_specs=[whole(ps), whole(pt), tall(2048), tall(2048)],
        out_specs=[tall(512)] * 2,
        name="grams",
    )(ps, pt, ts, tt)


SUMS = (
    pl.BlockSpec((1, 512), lambda i: (0, 0)),
    pl.BlockSpec((1, 512), lambda i: (0, 1)),
    pl.BlockSpec((1, 256), lambda i: (0, 4 + i)),
    pl.BlockSpec((1, 256), lambda i: (0, 7 + i)),
)


def inverse(total):
    return 1.0 / jnp.sqrt(total + epsilon)


def scaled(student, teacher, sums):
    inv_ps, inv_pt, inv_ts, inv_tt = (inverse(a[...] + b[...]) for a, b in zip(sums[:4], sums[4:]))
    scale = column(inv_ts, 4)
    near = student[...] * inv_ps * scale
    return near, near - teacher[...] * inv_pt * column(inv_tt, 4), inv_ps, scale


def part_kernel(student, teacher, *refs):
    refs[8][...] = scaled(student, teacher, refs[:8])[1].astype(bf16)


def part_of(student, teacher, mine, other):
    return pl.pallas_call(
        part_kernel,
        grid=(3,),
        out_shape=shape((768, 512), bf16),
        in_specs=[tall(512)] * 2 + [*SUMS, *SUMS],
        out_specs=tall(512),
        name="part",
    )(student, teacher, *([mine] * 4), *([other] * 4))


def mismatch_kernel(student, teacher, *refs):
    partner, doubled, weighted, loss, sides = refs[8:]
    step = pl.program_id(0)
    near, part, inv_ps, scale = scaled(student, teacher, refs[:8])
    mismatch = part + partner[...].astype(f32)
    twice = 2.0 * mismatch
    doubled[...] = (twice * inv_ps).astype(bf16)
    weighted[...] = (twice * scale).astype(bf16).T
    product = twice * near

    @pl.when(step == 0)
    def _():
        loss[...] = jnp.zeros_like(loss)
        sides[...] = jnp.zeros_like(sides)

    loss[...] += jnp.sum(mismatch * mismatch, axis=0, keepdims=True)
    sides[:, :512] += jnp.sum(product, axis=0, keepdims=True)
    sides[:, pl.ds(pl.multiple_of(512 + step * 256, 256), 256)] = to_row(fold_lanes(product))


def mismatch_of(student, teacher, mine, other, partner):
    return pl.pallas_call(
        mismatch_kernel,
        grid=(3,),
        out_shape=[shape((768, 512), bf16), shape((512, 768), bf16), shape((1, 512), f32), shape((1, 1280), f32)],
        in_specs=[tall(512)] * 2 + [*SUMS, *SUMS] + [tall(512)],
        out_specs=[
            tall(512),
            pl.BlockSpec((512, 256), lambda i: (0, i)),
            pl.BlockSpec((1, 512), lambda i: (0, 0)),
            pl.BlockSpec((1, 1280), lambda i: (0, 0)),
        ],
        name="mismatch",
    )(student, teacher, *([mine] * 4), *([other] * 4), partner)


def pick(weighted, core, ts):
    return jnp.dot(weighted[:, core].reshape(256, 768), ts[...], preferred_element_type=f32)


def away_kernel(core, weighted, ts, away):
    away[...] = pick(weighted, 1 - core[0], ts).astype(bf16)


def away_of(core, weighted, ts):
    return pl.pallas_call(
        away_kernel,
        grid=(4,),
        out_shape=shape((256, 2048), bf16),
        in_specs=[SMEM, whole(weighted), strip(ts)],
        out_specs=pl.BlockSpec((256, 512), lambda i: (0, i)),
        name="away",
    )(core, weighted, ts)


def join_kernel(core, weighted, ts, away, mine, other, out):
    step = pl.program_id(0)

    @pl.when(step < 4)
    def _():
        total = pick(weighted, core[0], ts) + away[...].astype(f32)
        out[...] = total.astype(bf16).reshape(16, 16, 512)

    @pl.when(step == 4)
    def _():
        stats = mine[...] + other[...]
        lane = lax.broadcasted_iota(jnp.int32, (512, 128), 1)
        tile = jnp.zeros((512, 128), f32)
        for row in range(2):
            total = column(stats[row : row + 1], 1)
            high = total.astype(bf16).astype(f32)
            tile = jnp.where(lane == 2 * row, high, jnp.where(lane == 2 * row + 1, total - high, tile))
        tile = tile.reshape(16, 2, 16, 128)
        out[:, :, :128] = jnp.where(core[0] == 0, tile[:, 0], tile[:, 1]).astype(bf16)


def join_of(core, weighted, ts, away, mine, other):
    return pl.pallas_call(
        join_kernel,
        grid=(5,),
        out_shape=shape((16, 16, 2176), bf16),
        in_specs=[SMEM, whole(weighted), strip(ts, last=3), strip(away, last=3), whole(mine), whole(other)],
        out_specs=pl.BlockSpec((16, 16, 512), lambda i: (0, 0, i)),
        name="join",
    )(core, weighted, ts, away, mine, other)


def final_kernel(spread, ps, inverses, loss, out):
    total = spread[0].astype(f32)
    for i in range(1, 16):
        total += spread[i].astype(f32)
    term, stats = total[:, :2048], total[:, 2048:]
    along = stats[:, 2:3] + stats[:, 3:4]
    unit = ps[...].astype(f32) * inverses[...]
    out[...] = ((term - unit * along) * inverses[...]).astype(bf16)
    turned = jnp.concatenate([stats, jnp.zeros((112, 128), f32)], axis=0).T
    loss[...] = (turned[0:1] + turned[1:2])[:, :16]


def final(spread, ps, inverses):
    return pl.pallas_call(
        final_kernel,
        out_shape=[shape((1, 16), f32), shape((16, 2048), bf16)],
        name="final",
    )(spread, ps, inverses)


def token_kernel(place, d0, dl, dr, do, ps, *refs):
    pieces, (ts, mine, other, a0, a1, a2, a3, out, work, twice) = refs[:12], refs[12:]
    deep, core = place[0], place[1]

    @pl.when(pl.program_id(0) == 0)
    def _():
        for i, ref in enumerate((d0, dl, dr, do)):
            twice[:, i * 512 : i * 512 + 512] = ref[...]

    work[:512] = ps[...]
    for order, (a, b) in enumerate(((deep, core), (1 - deep, core), (deep, 1 - core), (1 - deep, 1 - core))):
        for side in range(3):
            start = pl.multiple_of(512 * side + 512 + (a * 2 + b) * 128, 128)
            work[pl.ds(start, 128)] = pieces[order * 3 + side][...]
    total = jnp.dot(twice[...], work[...], preferred_element_type=f32)
    inv_ts = inverse(mine[...] + other[...])[:, 1024:1792]
    along = a0[...] + a1[...] + a2[...] + a3[...]
    copies = ts.shape[1] // 128
    out[...] = (total * column(inv_ts, copies) - ts[...].astype(f32) * column(inv_ts * inv_ts * along, copies)).astype(bf16)


def token_grad(place, doubled, ps, pieces, ts, mine, other, along):
    return pl.pallas_call(
        token_kernel,
        grid=(4,),
        out_shape=shape(ts.shape, bf16),
        in_specs=[SMEM]
        + [whole(a) for a in doubled]
        + [strip(a) for a in (ps, *pieces, ts)]
        + [whole(a) for a in (mine, other, *along)],
        out_specs=strip(ts),
        scratch_shapes=[pltpu.VMEM((2048, 512), bf16), pltpu.VMEM((768, 2048), bf16)],
        name="tokens",
    )(place, *doubled, ps, *pieces, ts, mine, other, *along)


def local(panel_student, panel_teacher, tokens_student, tokens_teacher):
    col = lax.axis_index("col")
    deep, core = (col // 2) % 2, col % 2
    place = jnp.stack([deep, core]).astype(jnp.int32)
    index = core.astype(jnp.int32)[None]
    features = (panel_student, panel_teacher, tokens_student, tokens_teacher)

    mine = norms(*features)
    other = feat_swap(mine)
    student, teacher = grams(*features)
    part = part_of(student, teacher, mine, other)
    held, part = lax.optimization_barrier((panel_student, part))
    partner = feat_swap(part)

    quarter = lax.dynamic_slice_in_dim(held, (deep * 2 + core) * 128, 128, 0)
    left = row_shift(quarter, 1)
    right = row_shift(quarter, 3)
    far = row_shift(quarter, 2)
    first = (left, right, far)
    second = (deep_shift(left, 1), deep_shift(right, 7), deep_shift(far, 1))
    third = tuple(core_swap(a) for a in first)
    fourth = tuple(core_swap(a) for a in second)
    pieces = first + second + third + fourth

    doubled, weighted, loss, sides = mismatch_of(student, teacher, mine, other, partner)
    gathered = (doubled, row_shift(doubled, 1), row_shift(doubled, 3), row_shift(doubled, 2))
    weighted = weighted.reshape(16, 2, 16, 768)
    away = away_of(index, weighted, tokens_student)
    away = core_swap(away)

    sides += feat_swap(sides)
    stats = jnp.concatenate([loss, sides[:, :512]], axis=0)
    stats_other = core_swap(stats)
    along = sides[:, 512:]
    along = (along,) + tuple(row_shift(along, i) for i in (1, 2, 3))

    joined = join_of(index, weighted, tokens_student, away, stats, stats_other)
    groups = [[a * 16 + z * 2 + k for a in range(2) for z in range(8)] for k in range(2)]
    spread = lax.all_to_all(joined, "col", 0, 0, axis_index_groups=groups, tiled=True)

    grad_tokens = token_grad(place, gathered, panel_student, pieces, tokens_student, mine, other, along)

    rows = lambda a: lax.dynamic_slice_in_dim(a, col * 16, 16, 0)
    inv_rows = inverse(rows(mine[0]) + rows(other[0]))[:, None]
    row_loss, grad_panel = final(spread, rows(panel_student), inv_rows)
    return (row_loss.reshape(16), grad_panel, grad_tokens)


def solution(mesh):
    placed = (P("row", "feat"), P("row", "feat"), P("col", "feat"), P("col", "feat"))
    return jax.shard_map(
        local,
        mesh=mesh,
        in_specs=placed,
        out_specs=(P(("row", "col")), P(("row", "col"), "feat"), P("col", "feat")),
        check_vma=False,
    )
```

```python
import jax
import jax.numpy as jnp
from jax import lax
from jax.experimental import pallas as pl
from jax.experimental.pallas import tpu as pltpu
from jax.sharding import PartitionSpec as P


epsilon = 1e-06
bf16, f32 = jnp.bfloat16, jnp.float32
SMEM = pl.BlockSpec(memory_space=pltpu.SMEM)


def row_shift(x, by):
    return lax.ppermute(x, "row", [(i, (i + by) % 4) for i in range(4)])


def feat_swap(x):
    return lax.ppermute(x, "feat", [(0, 1), (1, 0)])


def col_move(x, move):
    def target(c):
        a, z, k = move(c // 16, (c // 2) % 8, c % 2)
        return a * 16 + z * 2 + k

    return lax.ppermute(x, "col", [(c, target(c)) for c in range(32)])


def core_swap(x):
    return col_move(x, lambda a, z, k: (a, z, 1 - k))


def deep_shift(x, by):
    return col_move(x, lambda a, z, k: (a, (z + by) % 8, k))


def fold_lanes(x):
    return sum(x[:, i : i + 128] for i in range(0, x.shape[1], 128))


def to_row(x):
    return jnp.sum(x.T, axis=0, keepdims=True)


def column(row, copies):
    tall = jnp.broadcast_to(row, (128, row.shape[1])).T
    return jnp.concatenate([tall] * copies, axis=1)


def shape(dims, dtype):
    return jax.ShapeDtypeStruct(dims, dtype)


VMEM = pl.BlockSpec(memory_space=pltpu.VMEM)


def room(mib):
    return pltpu.CompilerParams(vmem_limit_bytes=mib << 20)


def near_core(*arrays):
    return tuple(pltpu.with_memory_space_constraint(a, pltpu.VMEM) for a in arrays)


def far_core(*arrays):
    return tuple(pltpu.with_memory_space_constraint(a, pltpu.HBM) for a in arrays)


def strip(a, width=512):
    return pl.BlockSpec((a.shape[0], width), lambda i: (0, i))


def whole(a):
    return pl.BlockSpec(a.shape, lambda i: (0,) * len(a.shape))


def cut(step, width=512):
    return pl.ds(pl.multiple_of(step * width, width), width)


def norm_kernel(deep, core, ps, pt, ts, tt, sums, quarter, *refs):
    held, squares = refs[:4], refs[4]
    step = pl.program_id(0)
    quarter[:, cut(step)] = ps[cut(deep[0] * 2 + core[0], 128)]

    @pl.when(step == 0)
    def _():
        squares[...] = jnp.zeros_like(squares)

    start = 0
    for ref, copy in zip((ps, pt, ts, tt), held):
        for row in range(0, ref.shape[0], 128):
            block = ref[row : row + 128]
            copy[row : row + 128, cut(step)] = block
            values = block.astype(f32)
            squares[start : start + 128] += fold_lanes(values * values)
            start += 128

    @pl.when(step == pl.num_programs(0) - 1)
    def _():
        sums[...] = to_row(squares[...])


def norms(deep, core, *features):
    return pl.pallas_call(
        norm_kernel,
        grid=(4,),
        out_shape=[pltpu.VMEM((1, 2560), f32), pltpu.VMEM((128, 2048), bf16)]
        + [pltpu.VMEM(a.shape, bf16) for a in features],
        in_specs=[SMEM] * 2 + [strip(a) for a in features],
        out_specs=[VMEM] * 6,
        scratch_shapes=[pltpu.VMEM((2560, 128), f32)],
        compiler_params=room(12),
        name="norms",
    )(deep, core, *far_core(*features))


def gram_kernel(ps, pt, ts, tt, student, teacher):
    def inner(left, right):
        return lax.dot_general(left, right[...], (((1,), (1,)), ((), ())), preferred_element_type=f32)

    rows = cut(pl.program_id(0), 256)
    student[rows] = inner(ts[rows], ps)
    teacher[rows] = inner(tt[rows], pt)


def grams(*features):
    return pl.pallas_call(
        gram_kernel,
        grid=(3,),
        out_shape=[pltpu.VMEM((768, 512), f32)] * 2,
        in_specs=[VMEM] * 4,
        out_specs=[VMEM] * 2,
        compiler_params=room(12),
        name="grams",
    )(*near_core(*features))


def inverse(total):
    return 1.0 / jnp.sqrt(total + epsilon)


def inverses(mine, other):
    invs = inverse(mine[...] + other[...])
    return invs[:, :512], invs[:, 512:1024], column(invs[:, 1024:1792], 1), column(invs[:, 1792:], 1)


def wide(x):
    return jnp.concatenate([x] * 4, axis=1)


def part_kernel(student, teacher, mine, other, out):
    inv_ps, inv_pt, inv_ts, inv_tt = inverses(mine, other)
    for row in range(0, 768, 64):
        rows = slice(row, row + 64)
        near = student[rows] * inv_ps * wide(inv_ts[rows])
        out[rows] = (near - teacher[rows] * inv_pt * wide(inv_tt[rows])).astype(bf16)


def part_of(*arrays):
    return pl.pallas_call(
        part_kernel,
        out_shape=pltpu.VMEM((768, 512), bf16),
        in_specs=[VMEM] * 4,
        out_specs=VMEM,
        compiler_params=room(12),
        name="part",
    )(*near_core(*arrays))


def mismatch_kernel(student, teacher, mine, other, partner, doubled, weighted, loss, sides):
    inv_ps, inv_pt, inv_ts, inv_tt = inverses(mine, other)
    losses = jnp.zeros((1, 512), f32)
    products = jnp.zeros((1, 512), f32)
    for row in range(0, 768, 128):
        rows = slice(row, row + 128)
        scale = wide(inv_ts[rows])
        near = student[rows] * inv_ps * scale
        part = near - teacher[rows] * inv_pt * wide(inv_tt[rows])
        mismatch = part + partner[rows].astype(f32)
        twice = 2.0 * mismatch
        doubled[rows] = (twice * inv_ps).astype(bf16)
        weighted[:, rows] = (twice * scale).astype(bf16).T
        product = twice * near
        losses += jnp.sum(mismatch * mismatch, axis=0, keepdims=True)
        products += jnp.sum(product, axis=0, keepdims=True)
        sides[:, 512 + row : 640 + row] = to_row(fold_lanes(product))
    loss[...] = losses
    sides[:, :512] = products


def mismatch_of(*arrays):
    return pl.pallas_call(
        mismatch_kernel,
        out_shape=[
            pltpu.VMEM((768, 512), bf16),
            pltpu.VMEM((512, 768), bf16),
            pltpu.VMEM((1, 512), f32),
            pltpu.VMEM((1, 1280), f32),
        ],
        in_specs=[VMEM] * 5,
        out_specs=[VMEM] * 4,
        compiler_params=room(12),
        name="mismatch",
    )(*near_core(*arrays))


def pick(weighted, core, ts, step):
    return jnp.dot(weighted[:, core].reshape(256, 768), ts[:, cut(step)], preferred_element_type=f32)


def away_kernel(core, weighted, ts, away):
    step = pl.program_id(0)
    away[:, cut(step)] = pick(weighted, 1 - core[0], ts, step).astype(bf16)


def away_of(core, *arrays):
    return pl.pallas_call(
        away_kernel,
        grid=(4,),
        out_shape=pltpu.VMEM((256, 2048), bf16),
        in_specs=[SMEM] + [VMEM] * 2,
        out_specs=VMEM,
        compiler_params=room(12),
        name="away",
    )(core, *near_core(*arrays))


def join_kernel(core, weighted, ts, away, mine, other, out):
    step = pl.program_id(0)

    @pl.when(step < 4)
    def _():
        total = pick(weighted, core[0], ts, step) + away[:, cut(step)].astype(f32)
        out[...] = total.astype(bf16).reshape(16, 16, 512)

    @pl.when(step == 4)
    def _():
        stats = mine[...] + other[...]
        lane = lax.broadcasted_iota(jnp.int32, (512, 128), 1)
        tile = jnp.zeros((512, 128), f32)
        for row in range(2):
            total = column(stats[row : row + 1], 1)
            high = total.astype(bf16).astype(f32)
            tile = jnp.where(lane == 2 * row, high, jnp.where(lane == 2 * row + 1, total - high, tile))
        tile = tile.reshape(16, 2, 16, 128)
        out[:, :, :128] = jnp.where(core[0] == 0, tile[:, 0], tile[:, 1]).astype(bf16)


def join_of(core, *arrays):
    return pl.pallas_call(
        join_kernel,
        grid=(5,),
        out_shape=shape((16, 16, 2176), bf16),
        in_specs=[SMEM] + [VMEM] * 5,
        out_specs=pl.BlockSpec((16, 16, 512), lambda i: (0, 0, i)),
        compiler_params=room(12),
        name="join",
    )(core, *near_core(*arrays))


def final_kernel(spread, ps, inverses, loss, out):
    def total(lanes):
        return sum(spread[i, :, lanes].astype(f32) for i in range(16))

    stats = total(slice(2048, 2176))
    along = stats[:, 2:3] + stats[:, 3:4]
    for lane in range(0, 2048, 512):
        lanes = slice(lane, lane + 512)
        unit = ps[:, lanes].astype(f32) * inverses[...]
        out[:, lanes] = ((total(lanes) - unit * along) * inverses[...]).astype(bf16)
    turned = jnp.concatenate([stats, jnp.zeros((112, 128), f32)], axis=0).T
    loss[...] = (turned[0:1] + turned[1:2])[:, :16]


def final(*arrays):
    return pl.pallas_call(
        final_kernel,
        out_shape=[shape((1, 16), f32), shape((16, 2048), bf16)],
        in_specs=[VMEM] * 3,
        out_specs=[VMEM] * 2,
        compiler_params=room(12),
        name="final",
    )(*near_core(*arrays))


def token_kernel(deep, core, d0, dl, dr, do, ps, *refs):
    pieces, (ts, mine, other, a0, a1, a2, a3, out, work, twice) = refs[:12], refs[12:]
    deep, core = deep[0], core[0]

    @pl.when(pl.program_id(0) == 0)
    def _():
        for i, ref in enumerate((d0, dl, dr, do)):
            twice[:, i * 512 : i * 512 + 512] = ref[...]

    work[:512] = ps[...]
    for order, (a, b) in enumerate(((deep, core), (1 - deep, core), (deep, 1 - core), (1 - deep, 1 - core))):
        for side in range(3):
            start = pl.multiple_of(512 * side + 512 + (a * 2 + b) * 128, 128)
            work[pl.ds(start, 128)] = pieces[order * 3 + side][...]
    total = jnp.dot(twice[...], work[...], preferred_element_type=f32)
    inv_ts = inverse(mine[...] + other[...])[:, 1024:1792]
    along = a0[...] + a1[...] + a2[...] + a3[...]
    copies = ts.shape[1] // 128
    out[...] = (total * column(inv_ts, copies) - ts[...].astype(f32) * column(inv_ts * inv_ts * along, copies)).astype(bf16)


def token_grad(deep, core, doubled, ps, pieces, ts, mine, other, along):
    return pl.pallas_call(
        token_kernel,
        grid=(4,),
        out_shape=shape(ts.shape, bf16),
        in_specs=[SMEM] * 2
        + [whole(a) for a in doubled]
        + [strip(a) for a in (ps, *pieces, ts)]
        + [whole(a) for a in (mine, other, *along)],
        out_specs=strip(ts),
        scratch_shapes=[pltpu.VMEM((2048, 512), bf16), pltpu.VMEM((768, 2048), bf16)],
        name="tokens",
    )(deep, core, *far_core(*doubled, ps, *pieces, ts), mine, other, *along)


def local(panel_student, panel_teacher, tokens_student, tokens_teacher):
    col = lax.axis_index("col")
    deep, core = (col // 2) % 2, col % 2
    parity, index = deep.astype(jnp.int32)[None], core.astype(jnp.int32)[None]
    features = (panel_student, panel_teacher, tokens_student, tokens_teacher)

    mine, quarter, *held = norms(parity, index, *features)
    other = feat_swap(mine)
    student, teacher = grams(*held)
    part = part_of(student, teacher, mine, other)
    partner = feat_swap(part)

    left = row_shift(quarter, 1)
    right = row_shift(quarter, 3)
    far = row_shift(quarter, 2)
    first = (left, right, far)
    second = (deep_shift(left, 1), deep_shift(right, 7), deep_shift(far, 1))
    third = tuple(core_swap(a) for a in first)
    fourth = tuple(core_swap(a) for a in second)
    pieces = first + second + third + fourth

    doubled, weighted, loss, sides = mismatch_of(student, teacher, mine, other, partner)
    gathered = (doubled, row_shift(doubled, 1), row_shift(doubled, 3), row_shift(doubled, 2))
    weighted = weighted.reshape(16, 2, 16, 768)
    away = away_of(index, weighted, held[2])
    away = core_swap(away)

    sides += feat_swap(sides)
    stats = jnp.concatenate([loss, sides[:, :512]], axis=0)
    stats_other = core_swap(stats)
    along = sides[:, 512:]
    along = (along,) + tuple(row_shift(along, i) for i in (1, 2, 3))

    joined = join_of(index, weighted, held[2], away, stats, stats_other)
    groups = [[a * 16 + z * 2 + k for a in range(2) for z in range(8)] for k in range(2)]
    spread = lax.all_to_all(joined, "col", 0, 0, axis_index_groups=groups, tiled=True)

    grad_tokens = token_grad(parity, index, gathered, panel_student, pieces, tokens_student, mine, other, along)

    rows = lambda a: lax.dynamic_slice_in_dim(a, col * 16, 16, 0)
    inv_rows = inverse(rows(mine[0]) + rows(other[0]))[:, None]
    row_loss, grad_panel = final(spread, rows(panel_student), inv_rows)
    return (row_loss.reshape(16), grad_panel, grad_tokens)


def solution(mesh):
    placed = (P("row", "feat"), P("row", "feat"), P("col", "feat"), P("col", "feat"))
    return jax.shard_map(
        local,
        mesh=mesh,
        in_specs=placed,
        out_specs=(P(("row", "col")), P(("row", "col"), "feat"), P("col", "feat")),
        check_vma=False,
    )
```

```python
import jax
import jax.numpy as jnp
from jax import lax
from jax.experimental import pallas as pl
from jax.experimental.pallas import tpu as pltpu
from jax.sharding import PartitionSpec as P


epsilon = 1e-06
bf16, f32 = jnp.bfloat16, jnp.float32
SMEM = pl.BlockSpec(memory_space=pltpu.SMEM)


def row_shift(x, by):
    return lax.ppermute(x, "row", [(i, (i + by) % 4) for i in range(4)])


def feat_swap(x):
    return lax.ppermute(x, "feat", [(0, 1), (1, 0)])


def col_move(x, move):
    def target(c):
        a, z, k = move(c // 16, (c // 2) % 8, c % 2)
        return a * 16 + z * 2 + k

    return lax.ppermute(x, "col", [(c, target(c)) for c in range(32)])


def core_swap(x):
    return col_move(x, lambda a, z, k: (a, z, 1 - k))


def near_swap(x):
    return col_move(x, lambda a, z, k: (1 - a, z, k))


def deep_shift(x, by):
    return col_move(x, lambda a, z, k: (a, (z + by) % 8, k))


def fold_lanes(x):
    return sum(x[:, i : i + 128] for i in range(0, x.shape[1], 128))


def to_row(x):
    return jnp.sum(x.T, axis=0, keepdims=True)


def column(row, copies):
    tall = jnp.broadcast_to(row, (128, row.shape[1])).T
    return jnp.concatenate([tall] * copies, axis=1)


def shape(dims, dtype):
    return jax.ShapeDtypeStruct(dims, dtype)


VMEM = pl.BlockSpec(memory_space=pltpu.VMEM)


def room(mib):
    return pltpu.CompilerParams(vmem_limit_bytes=mib << 20)


def near_core(*arrays):
    return tuple(pltpu.with_memory_space_constraint(a, pltpu.VMEM) for a in arrays)


def far_core(*arrays):
    return tuple(pltpu.with_memory_space_constraint(a, pltpu.HBM) for a in arrays)


def strip(a, width=512):
    return pl.BlockSpec((a.shape[0], width), lambda i: (0, i))


def cut(step, width=512):
    return pl.ds(pl.multiple_of(step * width, width), width)


def norm_kernel(deep, core, col, ps, pt, ts, tt, sums, quarter, few, *refs):
    held, squares = refs[:4], refs[4]
    step = pl.program_id(0)
    quarter[:, cut(step)] = ps[cut(deep[0] * 2 + core[0], 128)]
    few[:, cut(step)] = ps[cut(col[0], 16)]

    @pl.when(step == 0)
    def _():
        squares[...] = jnp.zeros_like(squares)

    start = 0
    for ref, copy in zip((ps, pt, ts, tt), held):
        for row in range(0, ref.shape[0], 128):
            block = ref[row : row + 128]
            copy[row : row + 128, cut(step)] = block
            values = block.astype(f32)
            squares[start : start + 128] += fold_lanes(values * values)
            start += 128

    @pl.when(step == pl.num_programs(0) - 1)
    def _():
        sums[...] = to_row(squares[...])


def norms(deep, core, col, *features):
    return pl.pallas_call(
        norm_kernel,
        grid=(4,),
        out_shape=[pltpu.VMEM((1, 2560), f32), pltpu.VMEM((128, 2048), bf16), pltpu.VMEM((16, 2048), bf16)]
        + [pltpu.VMEM(a.shape, bf16) for a in features],
        in_specs=[SMEM] * 3 + [strip(a) for a in features],
        out_specs=[VMEM] * 7,
        scratch_shapes=[pltpu.VMEM((2560, 128), f32)],
        compiler_params=room(12),
        name="norms",
    )(deep, core, col, *far_core(*features))


def gram_kernel(ps, pt, ts, tt, student, teacher):
    def inner(left, right):
        return lax.dot_general(left, right[...], (((1,), (1,)), ((), ())), preferred_element_type=f32)

    rows = cut(pl.program_id(0), 256)
    student[rows] = inner(ts[rows], ps)
    teacher[rows] = inner(tt[rows], pt)


def grams(*features):
    return pl.pallas_call(
        gram_kernel,
        grid=(3,),
        out_shape=[pltpu.VMEM((768, 512), f32)] * 2,
        in_specs=[VMEM] * 4,
        out_specs=[VMEM] * 2,
        compiler_params=room(12),
        name="grams",
    )(*near_core(*features))


def inverse(total):
    return 1.0 / jnp.sqrt(total + epsilon)


def inverses(mine, other):
    invs = inverse(mine[...] + other[...])
    return invs[:, :512], invs[:, 512:1024], column(invs[:, 1024:1792], 1), column(invs[:, 1792:], 1)


def wide(x):
    return jnp.concatenate([x] * 4, axis=1)


def part_kernel(student, teacher, mine, other, out):
    inv_ps, inv_pt, inv_ts, inv_tt = inverses(mine, other)
    for row in range(0, 768, 64):
        rows = slice(row, row + 64)
        near = student[rows] * inv_ps * wide(inv_ts[rows])
        out[rows] = (near - teacher[rows] * inv_pt * wide(inv_tt[rows])).astype(bf16)


def part_of(*arrays):
    return pl.pallas_call(
        part_kernel,
        out_shape=pltpu.VMEM((768, 512), bf16),
        in_specs=[VMEM] * 4,
        out_specs=VMEM,
        compiler_params=room(12),
        name="part",
    )(*near_core(*arrays))


def mismatch_kernel(student, teacher, mine, other, partner, doubled, weighted, sides):
    inv_ps, inv_pt, inv_ts, inv_tt = inverses(mine, other)
    losses = jnp.zeros((1, 512), f32)
    products = jnp.zeros((1, 512), f32)
    for row in range(0, 768, 128):
        rows = slice(row, row + 128)
        scale = wide(inv_ts[rows])
        near = student[rows] * inv_ps * scale
        part = near - teacher[rows] * inv_pt * wide(inv_tt[rows])
        mismatch = part + partner[rows].astype(f32)
        twice = 2.0 * mismatch
        doubled[rows] = (twice * inv_ps).astype(bf16)
        weighted[:, rows] = (twice * scale).astype(bf16).T
        product = twice * near
        losses += jnp.sum(mismatch * mismatch, axis=0, keepdims=True)
        products += jnp.sum(product, axis=0, keepdims=True)
        sides[:, 512 + row : 640 + row] = to_row(fold_lanes(product))
    sides[:, :512] = products
    sides[:, 1280:] = losses


def mismatch_of(*arrays):
    return pl.pallas_call(
        mismatch_kernel,
        out_shape=[
            pltpu.VMEM((768, 512), bf16),
            pltpu.VMEM((512, 768), bf16),
            pltpu.VMEM((1, 1792), f32),
        ],
        in_specs=[VMEM] * 5,
        out_specs=[VMEM] * 3,
        compiler_params=room(12),
        name="mismatch",
    )(*near_core(*arrays))


def pick(weighted, core, ts, step):
    return jnp.dot(weighted[:, core].reshape(256, 768), ts[:, cut(step)], preferred_element_type=f32)


def away_kernel(core, weighted, ts, away):
    step = pl.program_id(0)
    away[:, cut(step)] = pick(weighted, 1 - core[0], ts, step).astype(bf16)


def away_of(core, *arrays):
    return pl.pallas_call(
        away_kernel,
        grid=(4,),
        out_shape=pltpu.VMEM((256, 2048), bf16),
        in_specs=[SMEM] + [VMEM] * 2,
        out_specs=VMEM,
        compiler_params=room(12),
        name="away",
    )(core, *near_core(*arrays))


def join_kernel(core, weighted, ts, away, mine, other, out):
    step = pl.program_id(0)

    @pl.when(step < 4)
    def _():
        total = pick(weighted, core[0], ts, step) + away[:, cut(step)].astype(f32)
        out[...] = total.astype(bf16).reshape(16, 16, 512)

    @pl.when(step == 4)
    def _():
        stats = mine[...] + other[...]
        lane = lax.broadcasted_iota(jnp.int32, (512, 128), 1)
        tile = jnp.zeros((512, 128), f32)
        for row, part in enumerate((0.5 * stats[:, 1280:], stats[:, :512])):
            total = column(part, 1)
            high = total.astype(bf16).astype(f32)
            tile = jnp.where(lane == 2 * row, high, jnp.where(lane == 2 * row + 1, total - high, tile))
        tile = tile.reshape(16, 2, 16, 128)
        out[:, :, :128] = jnp.where(core[0] == 0, tile[:, 0], tile[:, 1]).astype(bf16)


def join_of(core, *arrays):
    return pl.pallas_call(
        join_kernel,
        grid=(5,),
        out_shape=pltpu.HBM((16, 16, 2176), bf16),
        in_specs=[SMEM] + [VMEM] * 5,
        out_specs=pl.BlockSpec((16, 16, 512), lambda i: (0, 0, i)),
        compiler_params=room(12),
        name="join",
    )(core, *near_core(*arrays))


def final_kernel(col, spread, few, mine, other, loss, out, tall):
    def total(lanes):
        return sum(spread[i, :, lanes].astype(f32) for i in range(16))

    tall[...] = column(inverse(mine[:, :512] + other[:, :512]), 1)
    inv_rows = wide(tall[cut(col[0], 16)])
    stats = total(slice(2048, 2176))
    along = stats[:, 2:3] + stats[:, 3:4]
    for lane in range(0, 2048, 512):
        lanes = slice(lane, lane + 512)
        unit = few[:, lanes].astype(f32) * inv_rows
        out[:, lanes] = ((total(lanes) - unit * along) * inv_rows).astype(bf16)
    turned = jnp.concatenate([stats, jnp.zeros((112, 128), f32)], axis=0).T
    loss[...] = (turned[0:1] + turned[1:2])[:, :16]


def final(col, *arrays):
    return pl.pallas_call(
        final_kernel,
        out_shape=[shape((1, 16), f32), shape((16, 2048), bf16)],
        in_specs=[SMEM] + [VMEM] * 4,
        out_specs=[VMEM] * 2,
        scratch_shapes=[pltpu.VMEM((512, 128), f32)],
        compiler_params=room(12),
        name="final",
    )(col, *near_core(*arrays))


def own_kernel(doubled, ps, out):
    out[:, cut(pl.program_id(0))] = jnp.dot(doubled[...], ps[...], preferred_element_type=f32)


def own_grad(doubled, ps):
    return pl.pallas_call(
        own_kernel,
        grid=(4,),
        out_shape=pltpu.VMEM((768, 2048), f32),
        in_specs=[VMEM, strip(ps)],
        out_specs=VMEM,
        compiler_params=room(12),
        name="own",
    )(*near_core(doubled), *far_core(ps))


def token_kernel(deep, core, dl, dr, do, *refs):
    pieces, (ts, own, mine, other, a0, a1, a2, a3, out, work, twice) = refs[:12], refs[12:]
    deep, core = deep[0], core[0]
    step = pl.program_id(0)

    @pl.when(step == 0)
    def _():
        for i, ref in enumerate((dl, dr, do)):
            twice[:, i * 512 : i * 512 + 512] = ref[...]

    for order, (a, b) in enumerate(((deep, core), (1 - deep, core), (deep, 1 - core), (1 - deep, 1 - core))):
        for side in range(3):
            start = pl.multiple_of(512 * side + (a * 2 + b) * 128, 128)
            work[pl.ds(start, 128)] = pieces[order * 3 + side][:, cut(step)]
    total = jnp.dot(twice[...], work[...], preferred_element_type=f32) + own[:, cut(step)]
    inv_ts = inverse(mine[...] + other[...])[:, 1024:1792]
    along = (a0[...] + a1[...] + a2[...] + a3[...])[:, 512:1280]
    scale, shade = wide(column(inv_ts, 1)), wide(column(inv_ts * inv_ts * along, 1))
    out[...] = (total * scale - ts[:, cut(step)].astype(f32) * shade).astype(bf16)


def token_grad(deep, core, *arrays):
    return pl.pallas_call(
        token_kernel,
        grid=(4,),
        out_shape=shape((768, 2048), bf16),
        in_specs=[SMEM] * 2 + [VMEM] * len(arrays),
        out_specs=pl.BlockSpec((768, 512), lambda i: (0, i)),
        scratch_shapes=[pltpu.VMEM((1536, 512), bf16), pltpu.VMEM((768, 1536), bf16)],
        compiler_params=room(18),
        name="tokens",
    )(deep, core, *near_core(*arrays))


def local(panel_student, panel_teacher, tokens_student, tokens_teacher):
    col = lax.axis_index("col")
    deep, core = (col // 16 + col // 2) % 2, col % 2
    parity, index, place = (a.astype(jnp.int32)[None] for a in (deep, core, col))
    features = (panel_student, panel_teacher, tokens_student, tokens_teacher)

    mine, quarter, few, *held = norms(parity, index, place, *features)
    other = feat_swap(mine)
    student, teacher = grams(*held)
    part = part_of(student, teacher, mine, other)
    partner = feat_swap(part)

    left = row_shift(quarter, 1)
    right = row_shift(quarter, 3)
    far = row_shift(quarter, 2)
    first = (left, right, far)
    second = (deep_shift(left, 1), deep_shift(right, 7), near_swap(far))
    third = tuple(core_swap(a) for a in first)
    fourth = tuple(core_swap(a) for a in second)
    pieces = first + second + third + fourth

    doubled, weighted, sides = mismatch_of(student, teacher, mine, other, partner)
    gathered = (row_shift(doubled, 1), row_shift(doubled, 3), row_shift(doubled, 2))
    weighted = weighted.reshape(16, 2, 16, 768)
    away = away_of(index, weighted, held[2])
    away = core_swap(away)

    sides += feat_swap(sides)
    stats_other = core_swap(sides)
    along = (sides,) + tuple(row_shift(sides, i) for i in (1, 2, 3))

    joined = join_of(index, weighted, held[2], away, sides, stats_other)
    groups = [[a * 16 + z * 2 + k for a in range(2) for z in range(8)] for k in range(2)]
    spread = lax.all_to_all(joined, "col", 0, 0, axis_index_groups=groups, tiled=True)

    own = own_grad(doubled, panel_student)
    grad_tokens = token_grad(parity, index, *gathered, *pieces, held[2], own, mine, other, *along)

    row_loss, grad_panel = final(place, spread, few, mine, other)
    return (row_loss.reshape(16), grad_panel, grad_tokens)


def solution(mesh):
    placed = (P("row", "feat"), P("row", "feat"), P("col", "feat"), P("col", "feat"))
    return jax.shard_map(
        local,
        mesh=mesh,
        in_specs=placed,
        out_specs=(P(("row", "col")), P(("row", "col"), "feat"), P("col", "feat")),
        check_vma=False,
    )
```
